32 devices in a mesh: wide: 8 (over z, x), narrow: 4 (over y, core).
Axes of the slice: x: 2, y: 2, z: 4, core: 2. Of those that a mesh axis runs over, the one named last changes fastest.
Arguments:
- states: bfloat16 [256, 262144], P('narrow', 'wide'), may hold values from -6 to 6
- obs_ens: bfloat16 [256, 32768], P('narrow', 'wide'), may hold values from -6 to 6
- obs_value: float32 [32768], P('wide'), may hold values from -6 to 6
- obs_prec: float32 [32768], P('wide'), may hold values from 0.1 to 1
- obs_pick: int32 [32, 1024], P('wide'), may hold values from 0 to 4607, as said below
- taper: float32 [32, 1024], P(('wide', 'narrow')), may hold values from 0.1 to 1
Outputs:
- analysis: bfloat16 [256, 262144], P('narrow', 'wide')
The draws below stay inside these ranges and needn't reach their ends.
Inputs may be any that keep to these rules, and one draw needn't show every extreme that they name: `obs_pick`: within a region the 1024 rows are distinct.
All inputs are finite; a program needn't handle non-finite values.
Results may differ from the reference program's by a relative error of at most 0.0057.
Values may be sent and summed in bfloat16 or wider, within the bound.
No kernel may reach another device: no remote copies, remote signals or barrier semaphores. Data moves between devices by JAX's collectives and lax.ppermute only.
A program may use at most 64 MiB of HBM per device.

```python
import math
import jax
import jax.numpy as jnp
from jax import lax

MEMBERS = 256
CELLS = 8192
OBS_W = 4096
HALO = 256
NPICK = 1024
ITERS = 6
REGIONS = 32
OBS = 32768
N_WIDE = 8
N_NARROW = 4


def draw_obs_pick(key, part):
    keys = jax.random.split(jax.random.fold_in(key, 17), REGIONS)

    def single(region_key):
        return jax.random.permutation(region_key, OBS_W + 2 * HALO)[:NPICK].astype(jnp.int32)
    return jax.vmap(single)(keys)


def block_levels(rng, shape, cuts, smallest, high):
    factor_of = 1.0
    for axis_at, shards_of in cuts:
        draws = jax.random.uniform(jax.random.fold_in(jax.random.fold_in(rng, 6), axis_at), (shards_of,), jnp.float32, smallest / len(cuts), high / len(cuts))
        factor_of = factor_of * jnp.repeat(jnp.exp(draws), shape[axis_at] // shards_of).reshape((-1,) + (1,) * (len(shape) - 1 - axis_at))
    return factor_of


def bell_draw(stream_key, dims, deviation, limit, pieces=(), kind=jnp.bfloat16):
    entries = deviation * jax.random.normal(stream_key, dims, jnp.float32)
    if pieces:
        entries = entries * block_levels(stream_key, dims, pieces, -0.22, 0.18)
    return jnp.clip(entries, -limit, limit).astype(kind)


def setup_inputs(seed: int = 0) -> dict:
    arg_keys = jax.random.split(jax.random.key(seed), 7)
    states = bell_draw(arg_keys[0], (MEMBERS, REGIONS * CELLS), 1.0, 6.0, ((0, 4), (1, 8)))
    obs_ens = bell_draw(arg_keys[1], (MEMBERS, OBS), 1.0, 6.0, ((0, 4), (1, 8)))
    obs_value = bell_draw(arg_keys[2], (OBS,), 1.0, 6.0, ((0, 8),), jnp.float32)
    obs_prec = jnp.clip(jnp.exp(math.log(1.0) - 2.3025851 * jax.random.uniform(arg_keys[3], (OBS,), jnp.float32) ** block_levels(arg_keys[3], (OBS,), ((0, 8),), -0.2, 0.2)), 0.1, 1.0)
    obs_pick = draw_obs_pick(jax.random.fold_in(arg_keys[6], 71), 0)
    taper = jnp.clip(0.1 + 0.9 * jax.random.uniform(arg_keys[5], (REGIONS, NPICK), jnp.float32) ** block_levels(arg_keys[5], (REGIONS, NPICK), ((0, 32),), -0.2, 0.2), 0.1, 1.0)
    return {"states": states, "obs_ens": obs_ens, "obs_value": obs_value, "obs_prec": obs_prec, "obs_pick": obs_pick, "taper": taper}


def analyse(ensemble, observed, precision, taper_row, regional):
    members = ensemble.shape[0]
    obs_mean = lax.optimization_barrier(jnp.mean(ensemble, axis=0))
    obs_pert = ensemble - obs_mean
    obs_weight = precision * taper_row
    scaled = (obs_pert * jnp.sqrt(obs_weight)).astype(jnp.bfloat16)
    identity = jnp.eye(members, dtype=jnp.float32)
    gram_sum = lax.dot_general(scaled, scaled, (((1,), (1,)), ((), ())), preferred_element_type=jnp.float32)
    precision_matrix = gram_sum + (members - 1.0) * identity
    forcing = jnp.dot(obs_pert, obs_weight * (observed - obs_mean), precision=lax.Precision.HIGHEST, preferred_element_type=jnp.float32)
    norm_scale = jnp.sqrt(jnp.sum(precision_matrix * precision_matrix))
    current = precision_matrix / norm_scale
    root_iter = identity
    for iteration in range(ITERS):
        middle = 1.5 * identity - 0.5 * jnp.dot(root_iter, current, precision=lax.Precision.HIGHEST, preferred_element_type=jnp.float32)
        current = jnp.dot(current, middle, precision=lax.Precision.HIGHEST, preferred_element_type=jnp.float32)
        root_iter = jnp.dot(middle, root_iter, precision=lax.Precision.HIGHEST, preferred_element_type=jnp.float32)
    inv_root = root_iter / jnp.sqrt(norm_scale)
    inner = jnp.dot(inv_root, forcing, precision=lax.Precision.HIGHEST, preferred_element_type=jnp.float32)
    mean_weights = jnp.dot(inv_root, inner, precision=lax.Precision.HIGHEST, preferred_element_type=jnp.float32)
    transform = (jnp.sqrt(members - 1.0) * inv_root + mean_weights[:, None]).astype(jnp.bfloat16)
    state_mean = lax.optimization_barrier(jnp.mean(regional.astype(jnp.float32), axis=0))
    state_pert = (regional.astype(jnp.float32) - state_mean).astype(jnp.bfloat16)
    mixed = lax.dot_general(transform, state_pert, (((0,), (0,)), ((), ())), preferred_element_type=jnp.float32)
    return (state_mean + mixed).astype(jnp.bfloat16)

def reference(states, obs_ens, obs_value, obs_prec, obs_pick, taper):
    total_obs = OBS_W * N_WIDE

    def region(index):
        band = index // N_NARROW
        columns = ((band * OBS_W - HALO + obs_pick[index]) % total_obs).astype(jnp.int32)
        ensemble = jnp.take(obs_ens, columns, axis=1).astype(jnp.float32)
        observed = jnp.take(obs_value, columns)
        precision = jnp.take(obs_prec, columns)
        regional = lax.dynamic_slice_in_dim(states, (index * CELLS).astype(jnp.int32), CELLS, 1)
        return analyse(ensemble, observed, precision, taper[index], regional)
    result = lax.map(region, jnp.arange(REGIONS, dtype=jnp.int32))
    members = states.shape[0]
    return jnp.transpose(result, (1, 0, 2)).reshape(members, REGIONS * CELLS)
```

```python
import functools

import jax
import jax.numpy as jnp
from jax import lax
from jax.experimental import pallas as pl
from jax.experimental.pallas import tpu as pltpu
from jax.sharding import PartitionSpec as P

HALO = 256
ITERS = 6
LANES = 128


VMEM = pl.BlockSpec(memory_space=pltpu.VMEM)
SMEM = pl.BlockSpec(memory_space=pltpu.SMEM)
HBM = pl.BlockSpec(memory_space=pltpu.HBM)


def params():
    return pltpu.CompilerParams(vmem_limit_bytes=16 << 20)


def cost(flops, moved):
    return pl.CostEstimate(flops=flops, bytes_accessed=moved, transcendentals=0)


def swap(array, d):
    n = lax.axis_size("narrow")
    return lax.ppermute(array, "narrow", [(i, i ^ d) for i in range(n)])


def halo(array, width, flip):
    size, n, length = lax.axis_size("wide"), lax.axis_size("narrow"), array.shape[1]
    up = [(w * n + i, (w + 1) % size * n + (i ^ flip)) for w in range(size) for i in range(n)]
    down = [(w * n + i, (w - 1) % size * n + (i ^ flip)) for w in range(size) for i in range(n)]
    before = lax.ppermute(array[:, length - width :], ("wide", "narrow"), up)
    after = lax.ppermute(array[:, :width], ("wide", "narrow"), down)
    return before, after


def pack_kernel(partners, cells, start, states_ref, *refs):
    count = len(partners)
    outs, sems = refs[:count], refs[count]
    pos = lax.axis_index("narrow")
    width = outs[0].shape[1]
    copies = []
    for k, d in enumerate(partners):
        column = pl.multiple_of((pos ^ d) * cells + start, LANES)
        copies.append(
            pltpu.make_async_copy(states_ref.at[:, pl.ds(column, width)], outs[k], sems.at[k])
        )
        copies[-1].start()
    for copy in copies:
        copy.wait()


def pack(states, partners, cells, start, width):
    rows = states.shape[0]
    count = len(partners)
    return pl.pallas_call(
        functools.partial(pack_kernel, partners, cells, start),
        in_specs=[HBM],
        out_specs=[VMEM] * count,
        out_shape=[jax.ShapeDtypeStruct((rows, width), jnp.bfloat16)] * count,
        scratch_shapes=[pltpu.SemaphoreType.DMA((count,))],
        compiler_params=params(),
        cost_estimate=cost(0, 4 * count * rows * width),
        name="pack",
    )(states)


def gather_kernel(pick_ref, *refs):
    parts, out_ref, table_ref, rows_ref = refs[:-3], refs[-3], refs[-2], refs[-1]
    base = 0
    for own_ref, other_ref in zip(parts[::2], parts[1::2]):
        for k in range(own_ref.shape[1] // LANES):
            block = jnp.concatenate(
                [
                    r[:, k * LANES : (k + 1) * LANES].astype(jnp.float32)
                    for r in (own_ref, other_ref)
                ],
                axis=0,
            )
            table_ref[base : base + LANES, :] = block.T
            base += LANES
    step = 16
    regions, used, _ = out_ref.shape
    pos = lax.axis_index("narrow")

    for region in range(regions):

        def move(g, carry):
            for u in range(step):
                j = g * step + u
                row = pick_ref[pos ^ (2 * region), j]
                rows_ref[pl.ds(j, 1), :] = table_ref[pl.ds(row, 1), :]
            return carry

        lax.fori_loop(0, used // step, move, 0)
        out_ref[region] = rows_ref[...].astype(jnp.bfloat16)


def gather(picks, parts):
    rows = parts[0].shape[0]
    window = sum(p.shape[1] for p in parts[::2])
    regions, used = picks.shape[0] // 2, picks.shape[1]
    return pl.pallas_call(
        gather_kernel,
        in_specs=[SMEM] + [VMEM] * len(parts),
        out_specs=VMEM,
        out_shape=jax.ShapeDtypeStruct((regions, used, 2 * rows), jnp.bfloat16),
        scratch_shapes=[
            pltpu.VMEM((window, 2 * rows), jnp.float32),
            pltpu.VMEM((used, 2 * rows), jnp.float32),
        ],
        compiler_params=params(),
        cost_estimate=cost(0, 16 * rows * (window + regions * used)),
        name="gather",
    )(picks, *parts)


def stats_kernel(pick_ref, taper_ref, *refs):
    parts, out_ref, table_ref = refs[:-2], refs[-2], refs[-1]
    base = 0
    for part in parts:
        for k in range(part.shape[1] // LANES):
            block = part[:, k * LANES : (k + 1) * LANES]
            block = jnp.concatenate([block, jnp.zeros((6, LANES), jnp.float32)], axis=0)
            table_ref[base : base + LANES, :] = block.T
            base += LANES
    step = 16
    used = out_ref.shape[0]
    pos = lax.axis_index("narrow")

    def move(g, carry):
        for u in range(step):
            j = g * step + u
            out_ref[pl.ds(j, 1), :] = table_ref[pl.ds(pick_ref[pos, j], 1), :]
        return carry

    lax.fori_loop(0, used // step, move, 0)
    for k in range(used // LANES):
        cut = slice(k * LANES, (k + 1) * LANES)
        column = jnp.broadcast_to(taper_ref[:, cut], (8, LANES)).T
        lane = lax.broadcasted_iota(jnp.int32, (LANES, 8), 1)
        out_ref[cut, :] = out_ref[cut, :] * jnp.where(lane == 1, column, 1.0)


def stats(picks, taper, parts):
    window = sum(p.shape[1] for p in parts)
    used = picks.shape[1]
    return pl.pallas_call(
        stats_kernel,
        in_specs=[SMEM] + [VMEM] * (1 + len(parts)),
        out_specs=VMEM,
        out_shape=jax.ShapeDtypeStruct((used, 8), jnp.float32),
        scratch_shapes=[pltpu.VMEM((window, 8), jnp.float32)],
        compiler_params=params(),
        cost_estimate=cost(0, 512 * (window + used)),
        name="stats",
    )(picks, taper, *parts)


def dot(a, b):
    return jnp.dot(a, b, precision=lax.Precision.HIGHEST, preferred_element_type=jnp.float32)


def transform_kernel(own_ref, stats_ref, *refs):
    others, out_ref = refs[:-1], refs[-1]
    ensemble = jnp.concatenate([own_ref[0]] + [r[...] for r in others], axis=1).astype(jnp.float32)
    members = ensemble.shape[1]
    value, weight = stats_ref[:, 0:1], stats_ref[:, 1:2]
    mean = jnp.sum(ensemble, axis=1, keepdims=True) * (1.0 / members)
    pert = ensemble - mean
    scaled = (pert * jnp.sqrt(weight)).astype(jnp.bfloat16)
    forcing = jnp.sum(pert * (weight * (value - mean)), axis=0, keepdims=True)
    row = lax.broadcasted_iota(jnp.int32, (members, members), 0)
    column = lax.broadcasted_iota(jnp.int32, (members, members), 1)
    identity = jnp.where(row == column, 1.0, 0.0)
    matrix = (members - 1.0) * identity + lax.dot_general(
        scaled, scaled, (((0,), (0,)), ((), ())), preferred_element_type=jnp.float32
    )
    squares = jnp.sum(jnp.sum(matrix * matrix, axis=0, keepdims=True), axis=1, keepdims=True)
    norm_scale = jnp.sqrt(squares)
    current = matrix / norm_scale
    root = 1.5 * identity - 0.5 * current
    current = dot(current, root)
    for iteration in range(1, ITERS):
        middle = 1.5 * identity - 0.5 * dot(root, current)
        if iteration < ITERS - 1:
            current = dot(current, middle)
        root = dot(middle, root)
    inv_root = root / jnp.sqrt(norm_scale)
    forcing = jnp.broadcast_to(forcing, (8, members))
    mean_weights = dot(dot(forcing, inv_root), inv_root)[0:1]
    out_ref[...] = (jnp.sqrt(jnp.float32(members - 1)) * inv_root + mean_weights).astype(jnp.bfloat16)


def transform(picked, stat, others):
    _, used, pair = picked.shape
    members = pair * (1 + len(others))
    return pl.pallas_call(
        transform_kernel,
        grid=(1,),
        in_specs=[
            pl.BlockSpec((1, used, pair), lambda i: (0, 0, 0)),
            pl.BlockSpec((used, 8), lambda i: (0, 0)),
        ]
        + [pl.BlockSpec((used, pair), lambda i: (0, 0))] * len(others),
        out_specs=pl.BlockSpec((members, members), lambda i: (0, 0)),
        out_shape=jax.ShapeDtypeStruct((members, members), jnp.bfloat16),
        compiler_params=params(),
        cost_estimate=cost(16 * 6 * 2 * members**3, 4 * used * members),
        name="transform",
    )(picked, stat, *others)


def apply_kernel(parts, at_ref, weights_ref, *refs):
    del at_ref
    sources, outs = refs[:parts], refs[-parts:]
    pieces = [r[...].astype(jnp.float32) for r in sources]
    rows = pieces[0].shape[0]
    total = sum(jnp.sum(p, axis=0, keepdims=True) for p in pieces)
    mean = total * (1.0 / (rows * parts))
    pert = jnp.concatenate([(p - mean).astype(jnp.bfloat16) for p in pieces], axis=0)
    mixed = jnp.dot(weights_ref[...], pert, preferred_element_type=jnp.float32)
    result = (mixed + mean).astype(jnp.bfloat16)
    for d in range(parts):
        outs[d][...] = result[d * rows : (d + 1) * rows]


def apply(weights, states, arrived, result, at, block):
    rows, width = arrived[0].shape
    parts = len(arrived) + 1
    members = rows * parts
    near = pl.BlockSpec((rows, block), lambda i, at: (0, at[0] + i))
    far = pl.BlockSpec((rows, block), lambda i, at: (0, i))
    given = [] if result is None else [result]
    return pl.pallas_call(
        functools.partial(apply_kernel, parts),
        grid_spec=pltpu.PrefetchScalarGridSpec(
            num_scalar_prefetch=1,
            grid=(width // block,),
            in_specs=[pl.BlockSpec((members, members), lambda i, at: (0, 0)), near]
            + [far] * (parts - 1)
            + [HBM] * len(given),
            out_specs=[near] + [far] * (parts - 1),
        ),
        out_shape=[jax.ShapeDtypeStruct(states.shape, jnp.bfloat16)]
        + [jax.ShapeDtypeStruct((rows, width), jnp.bfloat16)] * (parts - 1),
        input_output_aliases={2 + parts: 0} if given else {},
        compiler_params=params(),
        cost_estimate=cost(2 * members * members * width, 4 * members * width),
        name="apply",
    )(at, weights, states, *arrived, *given)


def place_kernel(cells, start, result_ref, *refs):
    del result_ref
    parts, out_ref, sems = refs[:-2], refs[-2], refs[-1]
    pos = lax.axis_index("narrow")
    copies = []
    for k, part in enumerate(parts):
        column = pl.multiple_of((pos ^ (k + 1)) * cells + start, LANES)
        copies.append(
            pltpu.make_async_copy(part, out_ref.at[:, pl.ds(column, part.shape[1])], sems.at[k])
        )
        copies[-1].start()
    for copy in copies:
        copy.wait()


def place(result, parts, cells, start):
    return pl.pallas_call(
        functools.partial(place_kernel, cells, start),
        in_specs=[HBM] + [VMEM] * len(parts),
        out_specs=HBM,
        out_shape=jax.ShapeDtypeStruct(result.shape, result.dtype),
        scratch_shapes=[pltpu.SemaphoreType.DMA((len(parts),))],
        input_output_aliases={0: 0},
        compiler_params=params(),
        cost_estimate=cost(0, sum(4 * p.size for p in parts)),
        name="place",
    )(result, *parts)


def body(states, obs_ens, obs_value, obs_prec, obs_pick, taper):
    n = lax.axis_size("narrow")
    pos = lax.axis_index("narrow")
    cells = states.shape[1] // n
    unit = cells // 8
    chunks = [(0, 4 * unit), (4 * unit, 2 * unit), (6 * unit, 2 * unit)]

    def send(source, partners, k):
        moved = []
        for d, part in zip(partners, pack(source, partners, cells, *chunks[k])):
            moved.append(swap(part, d))
        return moved

    far = list(range(2, n))
    incoming = [send(states, far, 0)]

    other = swap(obs_ens, 1)
    before, after = halo(obs_ens, HALO, 0)
    other_before, other_after = halo(obs_ens, HALO, 1)
    marks = jnp.stack([obs_value, obs_prec])
    mark_before, mark_after = halo(marks, HALO, 0)
    incoming[0] = send(states, [1], 0) + incoming[0]
    picked = gather(obs_pick, [before, other_before, obs_ens, other, after, other_after])
    states_late, picked = lax.optimization_barrier((states, picked))
    others = []
    for d in far[::2]:
        others.append(swap(picked[d // 2], d))
    for k in range(1, len(chunks)):
        moved = send(states_late, far, k)
        incoming.append(send(states_late, [1], k) + moved)

    weights = transform(picked, stats(obs_pick, taper, [mark_before, marks, mark_after]), others)

    result, outgoing = None, []
    for k, (start, width) in enumerate(chunks):
        at = jnp.reshape((pos * cells + start) // unit, (1,))
        result, *leaving = apply(weights, states, incoming[k], result, at, unit)
        moved = []
        for d, part in enumerate(leaving, 1):
            moved.append(swap(part, d))
        outgoing.append(moved)
    for (start, _), moved in zip(chunks, outgoing):
        result = place(result, moved, cells, start)
    return result


def solution(mesh):
    return jax.shard_map(
        body,
        mesh=mesh,
        in_specs=(
            P("narrow", "wide"),
            P("narrow", "wide"),
            P("wide"),
            P("wide"),
            P("wide", None),
            P(("wide", "narrow"), None),
        ),
        out_specs=P("narrow", "wide"),
        check_vma=False,
    )
```

```python
import functools

import jax
import jax.numpy as jnp
from jax import lax
from jax.experimental import pallas as pl
from jax.experimental.pallas import tpu as pltpu
from jax.sharding import PartitionSpec as P

HALO = 256
ITERS = 6
LANES = 128
FIRST = [(0, 2), (2, 3), (5, 3)]
OTHERS = [(0, 5), (5, 3)]
STEPS = [(0, 2), (2, 3), (5, 2), (7, 1)]


VMEM = pl.BlockSpec(memory_space=pltpu.VMEM)
SMEM = pl.BlockSpec(memory_space=pltpu.SMEM)
HBM = pl.BlockSpec(memory_space=pltpu.HBM)


def params():
    return pltpu.CompilerParams(vmem_limit_bytes=16 << 20)


def cost(flops, moved):
    return pl.CostEstimate(flops=flops, bytes_accessed=moved, transcendentals=0)


def swap(array, d):
    n = lax.axis_size("narrow")
    return lax.ppermute(array, "narrow", [(i, i ^ d) for i in range(n)])


def halo(last, first, flip):
    size, n = lax.axis_size("wide"), lax.axis_size("narrow")
    up = [(w * n + i, (w + 1) % size * n + (i ^ flip)) for w in range(size) for i in range(n)]
    down = [(w * n + i, (w - 1) % size * n + (i ^ flip)) for w in range(size) for i in range(n)]
    before = lax.ppermute(last, ("wide", "narrow"), up)
    after = lax.ppermute(first, ("wide", "narrow"), down)
    return before, after


def pack_kernel(partners, cells, start, states_ref, *refs):
    count = len(partners)
    outs, sems = refs[:count], refs[count]
    pos = lax.axis_index("narrow")
    width = outs[0].shape[1]
    copies = []
    for k, d in enumerate(partners):
        column = pl.multiple_of((pos ^ d) * cells + start, LANES)
        copies.append(
            pltpu.make_async_copy(states_ref.at[:, pl.ds(column, width)], outs[k], sems.at[k])
        )
        copies[-1].start()
    for copy in copies:
        copy.wait()


def pack(states, partners, cells, start, width):
    rows = states.shape[0]
    count = len(partners)
    return pl.pallas_call(
        functools.partial(pack_kernel, partners, cells, start),
        in_specs=[HBM],
        out_specs=[VMEM] * count,
        out_shape=[pltpu.VMEM((rows, width), jnp.bfloat16)] * count,
        scratch_shapes=[pltpu.SemaphoreType.DMA((count,))],
        compiler_params=params(),
        cost_estimate=cost(0, 4 * count * rows * width),
        name="pack",
    )(states)


def edges_kernel(*refs):
    outs = refs[-2:]
    rows = refs[0].shape[0]
    for k, out_ref in enumerate(outs):
        ens_ref, value_ref, prec_ref = refs[3 * k : 3 * k + 3]
        out_ref[:rows, :] = ens_ref[...].astype(jnp.float32)
        blank = jnp.zeros((6, out_ref.shape[1]), jnp.float32)
        out_ref[rows:, :] = jnp.concatenate([value_ref[...], prec_ref[...], blank], axis=0)


def edges(obs_ens, value, prec, width):
    rows, length = obs_ens.shape
    specs = [
        pl.BlockSpec((count, width), lambda i, at=at: (0, at))
        for at in (length // width - 1, 0)
        for count in (rows, 1, 1)
    ]
    shape = (rows + 8, width)
    return pl.pallas_call(
        edges_kernel,
        grid=(1,),
        in_specs=specs,
        out_specs=[pl.BlockSpec(shape, lambda i: (0, 0))] * 2,
        out_shape=[jax.ShapeDtypeStruct(shape, jnp.float32)] * 2,
        compiler_params=params(),
        cost_estimate=cost(0, 16 * rows * width),
        name="edges",
    )(*([obs_ens, value, prec] * 2))


def gather_kernel(regions, pick_ref, *refs):
    parts, outs, (table_ref, rows_ref) = refs[: -2 - regions], refs[-2 - regions : -2], refs[-2:]
    rows = table_ref.shape[1] // 2
    base = 0
    for own_ref, other_ref in zip(parts[::2], parts[1::2]):
        for k in range(own_ref.shape[1] // LANES):
            block = jnp.concatenate(
                [
                    r[:rows, k * LANES : (k + 1) * LANES].astype(jnp.float32)
                    for r in (own_ref, other_ref)
                ],
                axis=0,
            )
            table_ref[base : base + LANES, :] = block.T
            base += LANES
    step = 16
    used = rows_ref.shape[0]
    pos = lax.axis_index("narrow")

    for region in range(regions):

        def move(g, carry):
            for u in range(step):
                j = g * step + u
                row = pick_ref[pos ^ (2 * region), j]
                rows_ref[pl.ds(j, 1), :] = table_ref[pl.ds(row, 1), :]
            return carry

        lax.fori_loop(0, used // step, move, 0)
        outs[region][...] = rows_ref[...].astype(jnp.bfloat16)


def gather(picks, parts, rows):
    window = sum(p.shape[1] for p in parts[::2])
    regions, used = picks.shape[0] // 2, picks.shape[1]
    return pl.pallas_call(
        functools.partial(gather_kernel, regions),
        in_specs=[SMEM] + [VMEM] * len(parts),
        out_specs=[VMEM] * regions,
        out_shape=[jax.ShapeDtypeStruct((used, 2 * rows), jnp.bfloat16)] * regions,
        scratch_shapes=[
            pltpu.VMEM((window, 2 * rows), jnp.float32),
            pltpu.VMEM((used, 2 * rows), jnp.float32),
        ],
        compiler_params=params(),
        cost_estimate=cost(0, 16 * rows * (window + regions * used)),
        name="gather",
    )(picks, *parts)


def stats_kernel(pick_ref, taper_ref, before_ref, value_ref, prec_ref, after_ref, out_ref, table_ref):
    width = before_ref.shape[1]
    cuts = [slice(k, k + LANES) for k in range(0, width, LANES)]
    blocks = [before_ref[-8:, cut] for cut in cuts]
    blank = jnp.zeros((6, LANES), jnp.float32)
    for k in range(0, value_ref.shape[1], LANES):
        cut = slice(k, k + LANES)
        blocks.append(jnp.concatenate([value_ref[:, cut], prec_ref[:, cut], blank], axis=0))
    blocks += [after_ref[-8:, cut] for cut in cuts]
    for k, block in enumerate(blocks):
        table_ref[k * LANES : (k + 1) * LANES, :] = block.T
    step = 16
    used = out_ref.shape[0]
    pos = lax.axis_index("narrow")

    def move(g, carry):
        for u in range(step):
            j = g * step + u
            out_ref[pl.ds(j, 1), :] = table_ref[pl.ds(pick_ref[pos, j], 1), :]
        return carry

    lax.fori_loop(0, used // step, move, 0)
    for k in range(used // LANES):
        cut = slice(k * LANES, (k + 1) * LANES)
        column = jnp.broadcast_to(taper_ref[:, cut], (8, LANES)).T
        lane = lax.broadcasted_iota(jnp.int32, (LANES, 8), 1)
        out_ref[cut, :] = out_ref[cut, :] * jnp.where(lane == 1, column, 1.0)


def stats(picks, taper, parts):
    before, value, _, after = parts
    window = before.shape[1] + value.shape[1] + after.shape[1]
    used = picks.shape[1]
    return pl.pallas_call(
        stats_kernel,
        in_specs=[SMEM] + [VMEM] * (1 + len(parts)),
        out_specs=VMEM,
        out_shape=jax.ShapeDtypeStruct((used, 8), jnp.float32),
        scratch_shapes=[pltpu.VMEM((window, 8), jnp.float32)],
        compiler_params=params(),
        cost_estimate=cost(0, 512 * (window + used)),
        name="stats",
    )(picks, taper, *parts)


def dot(a, b):
    return jnp.dot(a, b, precision=lax.Precision.HIGHEST, preferred_element_type=jnp.float32)


def transform_kernel(own_ref, stats_ref, *refs):
    others, out_ref = refs[:-1], refs[-1]
    ensemble = jnp.concatenate([own_ref[...]] + [r[...] for r in others], axis=1).astype(jnp.float32)
    members = ensemble.shape[1]
    value, weight = stats_ref[:, 0:1], stats_ref[:, 1:2]
    mean = jnp.sum(ensemble, axis=1, keepdims=True) * (1.0 / members)
    pert = ensemble - mean
    scaled = (pert * jnp.sqrt(weight)).astype(jnp.bfloat16)
    forcing = jnp.sum(pert * (weight * (value - mean)), axis=0, keepdims=True)
    row = lax.broadcasted_iota(jnp.int32, (members, members), 0)
    column = lax.broadcasted_iota(jnp.int32, (members, members), 1)
    identity = jnp.where(row == column, 1.0, 0.0)
    matrix = (members - 1.0) * identity + lax.dot_general(
        scaled, scaled, (((0,), (0,)), ((), ())), preferred_element_type=jnp.float32
    )
    squares = jnp.sum(jnp.sum(matrix * matrix, axis=0, keepdims=True), axis=1, keepdims=True)
    norm_scale = jnp.sqrt(squares)
    current = matrix / norm_scale
    root = 1.5 * identity - 0.5 * current
    current = dot(current, root)
    for iteration in range(1, ITERS):
        middle = 1.5 * identity - 0.5 * dot(root, current)
        if iteration < ITERS - 1:
            current = dot(current, middle)
        root = dot(middle, root)
    inv_root = root / jnp.sqrt(norm_scale)
    forcing = jnp.broadcast_to(forcing, (8, members))
    mean_weights = dot(dot(forcing, inv_root), inv_root)[0:1]
    out_ref[...] = (jnp.sqrt(jnp.float32(members - 1)) * inv_root + mean_weights).astype(jnp.bfloat16)


def transform(picked, stat, others):
    used, pair = picked.shape
    members = pair * (1 + len(others))
    return pl.pallas_call(
        transform_kernel,
        grid=(1,),
        in_specs=[
            pl.BlockSpec((used, pair), lambda i: (0, 0)),
            pl.BlockSpec((used, 8), lambda i: (0, 0)),
        ]
        + [pl.BlockSpec((used, pair), lambda i: (0, 0))] * len(others),
        out_specs=pl.BlockSpec((members, members), lambda i: (0, 0)),
        out_shape=jax.ShapeDtypeStruct((members, members), jnp.bfloat16),
        compiler_params=params(),
        cost_estimate=cost(16 * 6 * 2 * members**3, 4 * used * members),
        name="transform",
    )(picked, stat, *others)


def apply_kernel(parts, at_ref, weights_ref, *refs):
    del at_ref
    sources, outs = refs[:parts], refs[-parts:]
    pieces = [r[...].astype(jnp.float32) for r in sources]
    rows = pieces[0].shape[0]
    total = sum(jnp.sum(p, axis=0, keepdims=True) for p in pieces)
    mean = total * (1.0 / (rows * parts))
    pert = jnp.concatenate([(p - mean).astype(jnp.bfloat16) for p in pieces], axis=0)
    mixed = jnp.dot(weights_ref[...], pert, preferred_element_type=jnp.float32)
    result = (mixed + mean).astype(jnp.bfloat16)
    for d in range(parts):
        outs[d][...] = result[d * rows : (d + 1) * rows]


def apply(weights, states, arrived, offsets, result, at, blocks, block):
    rows = states.shape[0]
    width = blocks * block
    parts = len(arrived) + 1
    members = rows * parts

    def far(offset):
        return pl.BlockSpec((rows, block), lambda i, at: (0, offset + i))

    near = pl.BlockSpec((rows, block), lambda i, at: (0, at[0] + i))
    given = [] if result is None else [result]
    return pl.pallas_call(
        functools.partial(apply_kernel, parts),
        grid_spec=pltpu.PrefetchScalarGridSpec(
            num_scalar_prefetch=1,
            grid=(blocks,),
            in_specs=[pl.BlockSpec((members, members), lambda i, at: (0, 0)), near]
            + [far(offset) for offset in offsets]
            + [HBM] * len(given),
            out_specs=[near] + [far(0)] * (parts - 1),
        ),
        out_shape=[jax.ShapeDtypeStruct(states.shape, jnp.bfloat16)]
        + [jax.ShapeDtypeStruct((rows, width), jnp.bfloat16)] * (parts - 1),
        input_output_aliases={2 + parts: 0} if given else {},
        compiler_params=params(),
        cost_estimate=cost(2 * members * members * width, 4 * members * width),
        name="apply",
    )(at, weights, states, *arrived, *given)


def place_kernel(cells, start, partners, result_ref, *refs):
    del result_ref
    parts, out_ref, sems = refs[:-2], refs[-2], refs[-1]
    pos = lax.axis_index("narrow")
    copies = []
    for k, part in enumerate(parts):
        column = pl.multiple_of((pos ^ partners[k]) * cells + start, LANES)
        copies.append(
            pltpu.make_async_copy(part, out_ref.at[:, pl.ds(column, part.shape[1])], sems.at[k])
        )
        copies[-1].start()
    for copy in copies:
        copy.wait()


def place(result, parts, cells, start, partners):
    return pl.pallas_call(
        functools.partial(place_kernel, cells, start, partners),
        in_specs=[HBM] + [VMEM] * len(parts),
        out_specs=HBM,
        out_shape=jax.ShapeDtypeStruct(result.shape, result.dtype),
        scratch_shapes=[pltpu.SemaphoreType.DMA((len(parts),))],
        input_output_aliases={0: 0},
        compiler_params=params(),
        cost_estimate=cost(0, sum(4 * p.size for p in parts)),
        name="place",
    )(result, *parts)


def body(states, obs_ens, obs_value, obs_prec, obs_pick, taper):
    n = lax.axis_size("narrow")
    pos = lax.axis_index("narrow")
    cells = states.shape[1] // n
    unit = cells // 8
    states = pltpu.with_memory_space_constraint(states, pltpu.HBM)

    arrived = {d: [] for d in range(1, n)}

    def send(partners, first, count):
        parts = pack(states, partners, cells, first * unit, count * unit)
        for d, part in zip(partners, parts):
            arrived[d].append((first, count, swap(part, d)))

    far = list(range(2, n))
    send(far[:1], *FIRST[0])
    send(far[1:], *OTHERS[0])
    send(far[:1], *FIRST[1])
    send(far, *OTHERS[1])
    send([1], 0, 8)

    other = swap(obs_ens, 1)
    value, prec = obs_value.reshape(1, -1), obs_prec.reshape(1, -1)
    last, first = edges(obs_ens, value, prec, HALO)
    before, after = halo(last, first, 0)
    other_before, other_after = halo(last, first, 1)
    rows = states.shape[0]
    picked = gather(obs_pick, [before, other_before, obs_ens, other, after, other_after], rows)
    others = []
    for d in far[::2]:
        others.append(swap(picked[d // 2], d))
    stat = stats(obs_pick, taper, [before, value, prec, after])
    weights = transform(picked[0], stat, others)

    result, outgoing = None, []
    for first, count in STEPS:
        at = jnp.reshape((pos * cells) // unit + first, (1,))
        parts, offsets = [], []
        for d in range(1, n):
            for base, units, part in arrived[d]:
                if base <= first < base + units:
                    parts.append(part)
                    offsets.append(first - base)
        result, *leaving = apply(weights, states, parts, offsets, result, at, count, unit)
        moved = []
        for d, part in enumerate(leaving, 1):
            moved.append(swap(part, d))
        outgoing.append((first, moved))
    for first, moved in outgoing:
        cut = n - 1 if first != STEPS[-1][0] else n - 2
        partners = list(range(1, n))
        result = place(result, moved[:cut], cells, first * unit, partners[:cut])
        if cut < n - 1:
            result = place(result, moved[cut:], cells, first * unit, partners[cut:])
    return result


def solution(mesh):
    return jax.shard_map(
        body,
        mesh=mesh,
        in_specs=(
            P("narrow", "wide"),
            P("narrow", "wide"),
            P("wide"),
            P("wide"),
            P("wide", None),
            P(("wide", "narrow"), None),
        ),
        out_specs=P("narrow", "wide"),
        check_vma=False,
    )
```

```python
import functools

import jax
import jax.numpy as jnp
from jax import lax
from jax.experimental import pallas as pl
from jax.experimental.pallas import tpu as pltpu
from jax.sharding import PartitionSpec as P

HALO = 256
ITERS = 6
LANES = 128
FIRST = [(0, 2), (2, 2), (4, 4)]
OTHERS = [(0, 4), (4, 4)]
STEPS = [(0, 2), (2, 2), (4, 3), (7, 1)]


VMEM = pl.BlockSpec(memory_space=pltpu.VMEM)
SMEM = pl.BlockSpec(memory_space=pltpu.SMEM)
HBM = pl.BlockSpec(memory_space=pltpu.HBM)


def params():
    return pltpu.CompilerParams(vmem_limit_bytes=16 << 20)


def cost(flops, moved):
    return pl.CostEstimate(flops=flops, bytes_accessed=moved, transcendentals=0)


def swap(array, d):
    n = lax.axis_size("narrow")
    return lax.ppermute(array, "narrow", [(i, i ^ d) for i in range(n)])


def halo(last, first, flip):
    size, n = lax.axis_size("wide"), lax.axis_size("narrow")
    up = [(w * n + i, (w + 1) % size * n + (i ^ flip)) for w in range(size) for i in range(n)]
    down = [(w * n + i, (w - 1) % size * n + (i ^ flip)) for w in range(size) for i in range(n)]
    before = lax.ppermute(last, ("wide", "narrow"), up)
    after = lax.ppermute(first, ("wide", "narrow"), down)
    return before, after


def pack_kernel(partners, cells, start, states_ref, *refs):
    count = len(partners)
    outs, sems = refs[:count], refs[count]
    pos = lax.axis_index("narrow")
    width = outs[0].shape[1]
    copies = []
    for k, d in enumerate(partners):
        column = pl.multiple_of((pos ^ d) * cells + start, LANES)
        copies.append(
            pltpu.make_async_copy(states_ref.at[:, pl.ds(column, width)], outs[k], sems.at[k])
        )
        copies[-1].start()
    for copy in copies:
        copy.wait()


def pack(states, partners, cells, start, width):
    rows = states.shape[0]
    count = len(partners)
    return pl.pallas_call(
        functools.partial(pack_kernel, partners, cells, start),
        in_specs=[HBM],
        out_specs=[VMEM] * count,
        out_shape=[pltpu.VMEM((rows, width), jnp.bfloat16)] * count,
        scratch_shapes=[pltpu.SemaphoreType.DMA((count,))],
        compiler_params=params(),
        cost_estimate=cost(0, 4 * count * rows * width),
        name="pack",
    )(states)


def edges_kernel(*refs):
    outs = refs[-2:]
    rows = refs[0].shape[0]
    for k, out_ref in enumerate(outs):
        ens_ref, value_ref, prec_ref = refs[3 * k : 3 * k + 3]
        out_ref[:rows, :] = ens_ref[...].astype(jnp.float32)
        blank = jnp.zeros((6, out_ref.shape[1]), jnp.float32)
        out_ref[rows:, :] = jnp.concatenate([value_ref[...], prec_ref[...], blank], axis=0)


def edges(obs_ens, value, prec, width):
    rows, length = obs_ens.shape
    specs = [
        pl.BlockSpec((count, width), lambda i, at=at: (0, at))
        for at in (length // width - 1, 0)
        for count in (rows, 1, 1)
    ]
    shape = (rows + 8, width)
    return pl.pallas_call(
        edges_kernel,
        grid=(1,),
        in_specs=specs,
        out_specs=[pl.BlockSpec(shape, lambda i: (0, 0))] * 2,
        out_shape=[jax.ShapeDtypeStruct(shape, jnp.float32)] * 2,
        compiler_params=params(),
        cost_estimate=cost(0, 16 * rows * width),
        name="edges",
    )(*([obs_ens, value, prec] * 2))


def gather_kernel(regions, pick_ref, *refs):
    parts, outs, (table_ref, rows_ref) = refs[: -2 - regions], refs[-2 - regions : -2], refs[-2:]
    rows = table_ref.shape[1] // 2
    base = 0
    for own_ref, other_ref in zip(parts[::2], parts[1::2]):
        for k in range(own_ref.shape[1] // LANES):
            block = jnp.concatenate(
                [
                    r[:rows, k * LANES : (k + 1) * LANES].astype(jnp.float32)
                    for r in (own_ref, other_ref)
                ],
                axis=0,
            )
            table_ref[base : base + LANES, :] = block.T
            base += LANES
    step = 16
    used = rows_ref.shape[0]
    pos = lax.axis_index("narrow")

    for region in range(regions):

        def move(g, carry):
            for u in range(step):
                j = g * step + u
                row = pick_ref[pos ^ (2 * region), j]
                rows_ref[pl.ds(j, 1), :] = table_ref[pl.ds(row, 1), :]
            return carry

        lax.fori_loop(0, used // step, move, 0)
        outs[region][...] = rows_ref[...].astype(jnp.bfloat16)


def gather(picks, parts, rows):
    window = sum(p.shape[1] for p in parts[::2])
    regions, used = picks.shape[0] // 2, picks.shape[1]
    return pl.pallas_call(
        functools.partial(gather_kernel, regions),
        in_specs=[SMEM] + [VMEM] * len(parts),
        out_specs=[VMEM] * regions,
        out_shape=[jax.ShapeDtypeStruct((used, 2 * rows), jnp.bfloat16)] * regions,
        scratch_shapes=[
            pltpu.VMEM((window, 2 * rows), jnp.float32),
            pltpu.VMEM((used, 2 * rows), jnp.float32),
        ],
        compiler_params=params(),
        cost_estimate=cost(0, 16 * rows * (window + regions * used)),
        name="gather",
    )(picks, *parts)


def stats_kernel(pick_ref, taper_ref, before_ref, value_ref, prec_ref, after_ref, out_ref, table_ref):
    width = before_ref.shape[1]
    cuts = [slice(k, k + LANES) for k in range(0, width, LANES)]
    blocks = [before_ref[-8:, cut] for cut in cuts]
    blank = jnp.zeros((6, LANES), jnp.float32)
    for k in range(0, value_ref.shape[1], LANES):
        cut = slice(k, k + LANES)
        blocks.append(jnp.concatenate([value_ref[:, cut], prec_ref[:, cut], blank], axis=0))
    blocks += [after_ref[-8:, cut] for cut in cuts]
    for k, block in enumerate(blocks):
        table_ref[k * LANES : (k + 1) * LANES, :] = block.T
    step = 16
    used = out_ref.shape[0]
    pos = lax.axis_index("narrow")

    def move(g, carry):
        for u in range(step):
            j = g * step + u
            out_ref[pl.ds(j, 1), :] = table_ref[pl.ds(pick_ref[pos, j], 1), :]
        return carry

    lax.fori_loop(0, used // step, move, 0)
    for k in range(used // LANES):
        cut = slice(k * LANES, (k + 1) * LANES)
        column = jnp.broadcast_to(taper_ref[:, cut], (8, LANES)).T
        lane = lax.broadcasted_iota(jnp.int32, (LANES, 8), 1)
        out_ref[cut, :] = out_ref[cut, :] * jnp.where(lane == 1, column, 1.0)


def stats(picks, taper, parts):
    before, value, _, after = parts
    window = before.shape[1] + value.shape[1] + after.shape[1]
    used = picks.shape[1]
    return pl.pallas_call(
        stats_kernel,
        in_specs=[SMEM] + [VMEM] * (1 + len(parts)),
        out_specs=VMEM,
        out_shape=jax.ShapeDtypeStruct((used, 8), jnp.float32),
        scratch_shapes=[pltpu.VMEM((window, 8), jnp.float32)],
        compiler_params=params(),
        cost_estimate=cost(0, 512 * (window + used)),
        name="stats",
    )(picks, taper, *parts)


def dot(a, b):
    return jnp.dot(a, b, precision=lax.Precision.HIGHEST, preferred_element_type=jnp.float32)


def transform_kernel(own_ref, stats_ref, *refs):
    others, out_ref = refs[:-1], refs[-1]
    ensemble = jnp.concatenate([own_ref[...]] + [r[...] for r in others], axis=1).astype(jnp.float32)
    members = ensemble.shape[1]
    value, weight = stats_ref[:, 0:1], stats_ref[:, 1:2]
    mean = jnp.sum(ensemble, axis=1, keepdims=True) * (1.0 / members)
    pert = ensemble - mean
    scaled = (pert * jnp.sqrt(weight)).astype(jnp.bfloat16)
    forcing = jnp.sum(pert * (weight * (value - mean)), axis=0, keepdims=True)
    row = lax.broadcasted_iota(jnp.int32, (members, members), 0)
    column = lax.broadcasted_iota(jnp.int32, (members, members), 1)
    identity = jnp.where(row == column, 1.0, 0.0)
    matrix = (members - 1.0) * identity + lax.dot_general(
        scaled, scaled, (((0,), (0,)), ((), ())), preferred_element_type=jnp.float32
    )
    squares = jnp.sum(jnp.sum(matrix * matrix, axis=0, keepdims=True), axis=1, keepdims=True)
    norm_scale = jnp.sqrt(squares)
    current = matrix / norm_scale
    root = 1.5 * identity - 0.5 * current
    current = dot(current, root)
    for iteration in range(1, ITERS):
        middle = 1.5 * identity - 0.5 * dot(root, current)
        if iteration < ITERS - 1:
            current = dot(current, middle)
        root = dot(middle, root)
    inv_root = root / jnp.sqrt(norm_scale)
    forcing = jnp.broadcast_to(forcing, (8, members))
    mean_weights = dot(dot(forcing, inv_root), inv_root)[0:1]
    out_ref[...] = (jnp.sqrt(jnp.float32(members - 1)) * inv_root + mean_weights).astype(jnp.bfloat16)


def transform(picked, stat, others):
    used, pair = picked.shape
    members = pair * (1 + len(others))
    return pl.pallas_call(
        transform_kernel,
        grid=(1,),
        in_specs=[
            pl.BlockSpec((used, pair), lambda i: (0, 0)),
            pl.BlockSpec((used, 8), lambda i: (0, 0)),
        ]
        + [pl.BlockSpec((used, pair), lambda i: (0, 0))] * len(others),
        out_specs=pl.BlockSpec((members, members), lambda i: (0, 0)),
        out_shape=jax.ShapeDtypeStruct((members, members), jnp.bfloat16),
        compiler_params=params(),
        cost_estimate=cost(16 * 6 * 2 * members**3, 4 * used * members),
        name="transform",
    )(picked, stat, *others)


def apply_kernel(parts, weights_ref, *refs):
    sources, outs = refs[:parts], refs[-parts:]
    pieces = [r[...].astype(jnp.float32) for r in sources]
    rows = pieces[0].shape[0]
    total = sum(jnp.sum(p, axis=0, keepdims=True) for p in pieces)
    mean = total * (1.0 / (rows * parts))
    pert = jnp.concatenate([(p - mean).astype(jnp.bfloat16) for p in pieces], axis=0)
    mixed = jnp.dot(weights_ref[...], pert, preferred_element_type=jnp.float32)
    result = (mixed + mean).astype(jnp.bfloat16)
    for d in range(parts):
        outs[d][...] = result[d * rows : (d + 1) * rows]


def apply(weights, states, arrived, offsets, result, first, blocks, block, stride):
    rows = states.shape[0]
    width = blocks * block
    parts = len(arrived) + 1
    members = rows * parts

    def far(offset):
        return pl.BlockSpec((rows, block), lambda i: (0, offset + i))

    near = pl.BlockSpec(
        (rows, block), lambda i: (0, lax.axis_index("narrow") * stride + first + i)
    )
    given = [] if result is None else [result]
    return pl.pallas_call(
        functools.partial(apply_kernel, parts),
        grid=(blocks,),
        in_specs=[pl.BlockSpec((members, members), lambda i: (0, 0)), near]
        + [far(offset) for offset in offsets]
        + [HBM] * len(given),
        out_specs=[near] + [far(0)] * (parts - 1),
        out_shape=[jax.ShapeDtypeStruct(states.shape, jnp.bfloat16)]
        + [pltpu.VMEM((rows, width), jnp.bfloat16)] * (parts - 1),
        input_output_aliases={1 + parts: 0} if given else {},
        compiler_params=params(),
        cost_estimate=cost(2 * members * members * width, 4 * members * width),
        name="apply",
    )(weights, states, *arrived, *given)


def place_kernel(cells, start, partners, result_ref, *refs):
    del result_ref
    parts, out_ref, sems = refs[:-2], refs[-2], refs[-1]
    pos = lax.axis_index("narrow")
    copies = []
    for k, part in enumerate(parts):
        column = pl.multiple_of((pos ^ partners[k]) * cells + start, LANES)
        copies.append(
            pltpu.make_async_copy(part, out_ref.at[:, pl.ds(column, part.shape[1])], sems.at[k])
        )
        copies[-1].start()
    for copy in copies:
        copy.wait()


def place(result, parts, cells, start, partners):
    return pl.pallas_call(
        functools.partial(place_kernel, cells, start, partners),
        in_specs=[HBM] + [VMEM] * len(parts),
        out_specs=HBM,
        out_shape=jax.ShapeDtypeStruct(result.shape, result.dtype),
        scratch_shapes=[pltpu.SemaphoreType.DMA((len(parts),))],
        input_output_aliases={0: 0},
        compiler_params=params(),
        cost_estimate=cost(0, sum(4 * p.size for p in parts)),
        name="place",
    )(result, *parts)


def body(states, obs_ens, obs_value, obs_prec, obs_pick, taper):
    n = lax.axis_size("narrow")
    cells = states.shape[1] // n
    unit = cells // 8
    states = pltpu.with_memory_space_constraint(states, pltpu.HBM)

    arrived = {d: [] for d in range(1, n)}

    def send(partners, first, count):
        parts = pack(states, partners, cells, first * unit, count * unit)
        for d, part in zip(partners, parts):
            arrived[d].append((first, count, swap(part, d)))

    far = list(range(2, n))
    send(far[:1], *FIRST[0])
    send(far[1:], *OTHERS[0])
    send(far[:1], *FIRST[1])
    send(far, *OTHERS[1])
    send([1], 0, 8)

    other = swap(obs_ens, 1)
    value, prec = obs_value.reshape(1, -1), obs_prec.reshape(1, -1)
    last, first = edges(obs_ens, value, prec, HALO)
    before, after = halo(last, first, 0)
    other_before, other_after = halo(last, first, 1)
    rows = states.shape[0]
    picked = gather(obs_pick, [before, other_before, obs_ens, other, after, other_after], rows)
    others = []
    for d in far[::2]:
        others.append(swap(picked[d // 2], d))
    stat = stats(obs_pick, taper, [before, value, prec, after])
    weights = transform(picked[0], stat, others)

    result, outgoing = None, []
    for first, count in STEPS:
        parts, offsets = [], []
        for d in range(1, n):
            for base, units, part in arrived[d]:
                if base <= first < base + units:
                    parts.append(part)
                    offsets.append(first - base)
        result, *leaving = apply(
            weights, states, parts, offsets, result, first, count, unit, cells // unit
        )
        moved = []
        for d, part in enumerate(leaving, 1):
            moved.append(swap(part, d))
        outgoing.append((first, moved))
    for first, moved in outgoing:
        cut = n - 1 if first != STEPS[-1][0] else n - 2
        partners = list(range(1, n))
        result = place(result, moved[:cut], cells, first * unit, partners[:cut])
        if cut < n - 1:
            result = place(result, moved[cut:], cells, first * unit, partners[cut:])
    return result


def solution(mesh):
    return jax.shard_map(
        body,
        mesh=mesh,
        in_specs=(
            P("narrow", "wide"),
            P("narrow", "wide"),
            P("wide"),
            P("wide"),
            P("wide", None),
            P(("wide", "narrow"), None),
        ),
        out_specs=P("narrow", "wide"),
        check_vma=False,
    )
```

```python
import functools

import jax
import jax.numpy as jnp
from jax import lax
from jax.experimental import pallas as pl
from jax.experimental.pallas import tpu as pltpu
from jax.sharding import PartitionSpec as P

HALO = 256
ITERS = 6
LANES = 128
FIRST = [(0, 1), (1, 4), (5, 3)]
OTHERS = [(0, 5), (5, 3)]
STEPS = [(0, 1), (1, 4), (5, 2), (7, 1)]


VMEM = pl.BlockSpec(memory_space=pltpu.VMEM)
SMEM = pl.BlockSpec(memory_space=pltpu.SMEM)
HBM = pl.BlockSpec(memory_space=pltpu.HBM)


def params():
    return pltpu.CompilerParams(vmem_limit_bytes=16 << 20)


def cost(flops, moved):
    return pl.CostEstimate(flops=flops, bytes_accessed=moved, transcendentals=0)


def swap(array, d):
    n = lax.axis_size("narrow")
    return lax.ppermute(array, "narrow", [(i, i ^ d) for i in range(n)])


def halo(last, first, flip):
    size, n = lax.axis_size("wide"), lax.axis_size("narrow")
    up = [(w * n + i, (w + 1) % size * n + (i ^ flip)) for w in range(size) for i in range(n)]
    down = [(w * n + i, (w - 1) % size * n + (i ^ flip)) for w in range(size) for i in range(n)]
    before = lax.ppermute(last, ("wide", "narrow"), up)
    after = lax.ppermute(first, ("wide", "narrow"), down)
    return before, after


def pack_kernel(partners, cells, start, states_ref, *refs):
    count = len(partners)
    outs, sems = refs[:count], refs[count]
    pos = lax.axis_index("narrow")
    width = outs[0].shape[1]
    copies = []
    for k, d in enumerate(partners):
        column = pl.multiple_of((pos ^ d) * cells + start, LANES)
        copies.append(
            pltpu.make_async_copy(states_ref.at[:, pl.ds(column, width)], outs[k], sems.at[k])
        )
        copies[-1].start()
    for copy in copies:
        copy.wait()


def pack(states, partners, cells, start, width):
    rows = states.shape[0]
    count = len(partners)
    return pl.pallas_call(
        functools.partial(pack_kernel, partners, cells, start),
        in_specs=[HBM],
        out_specs=[VMEM] * count,
        out_shape=[pltpu.VMEM((rows, width), jnp.bfloat16)] * count,
        scratch_shapes=[pltpu.SemaphoreType.DMA((count,))],
        compiler_params=params(),
        cost_estimate=cost(0, 4 * count * rows * width),
        name="pack",
    )(states)


def edges_kernel(*refs):
    outs = refs[-2:]
    rows = refs[0].shape[0]
    for k, out_ref in enumerate(outs):
        ens_ref, value_ref, prec_ref = refs[3 * k : 3 * k + 3]
        out_ref[:rows, :] = ens_ref[...].astype(jnp.float32)
        blank = jnp.zeros((6, out_ref.shape[1]), jnp.float32)
        out_ref[rows:, :] = jnp.concatenate([value_ref[...], prec_ref[...], blank], axis=0)


def edges(obs_ens, value, prec, width):
    rows, length = obs_ens.shape
    specs = [
        pl.BlockSpec((count, width), lambda i, at=at: (0, at))
        for at in (length // width - 1, 0)
        for count in (rows, 1, 1)
    ]
    shape = (rows + 8, width)
    return pl.pallas_call(
        edges_kernel,
        grid=(1,),
        in_specs=specs,
        out_specs=[pl.BlockSpec(shape, lambda i: (0, 0))] * 2,
        out_shape=[jax.ShapeDtypeStruct(shape, jnp.float32)] * 2,
        compiler_params=params(),
        cost_estimate=cost(0, 16 * rows * width),
        name="edges",
    )(*([obs_ens, value, prec] * 2))


def gather_kernel(regions, pick_ref, *refs):
    parts, outs, (table_ref, rows_ref) = refs[: -2 - regions], refs[-2 - regions : -2], refs[-2:]
    rows = table_ref.shape[1] // 2
    base = 0
    for own_ref, other_ref in zip(parts[::2], parts[1::2]):
        for k in range(own_ref.shape[1] // LANES):
            block = jnp.concatenate(
                [
                    r[:rows, k * LANES : (k + 1) * LANES].astype(jnp.float32)
                    for r in (own_ref, other_ref)
                ],
                axis=0,
            )
            table_ref[base : base + LANES, :] = block.T
            base += LANES
    step = 16
    used = rows_ref.shape[0]
    pos = lax.axis_index("narrow")

    for region in range(regions):

        def move(g, carry):
            for u in range(step):
                j = g * step + u
                row = pick_ref[pos ^ (2 * region), j]
                rows_ref[pl.ds(j, 1), :] = table_ref[pl.ds(row, 1), :]
            return carry

        lax.fori_loop(0, used // step, move, 0)
        outs[region][...] = rows_ref[...].astype(jnp.bfloat16)


def gather(picks, parts, rows):
    window = sum(p.shape[1] for p in parts[::2])
    regions, used = picks.shape[0] // 2, picks.shape[1]
    return pl.pallas_call(
        functools.partial(gather_kernel, regions),
        in_specs=[SMEM] + [VMEM] * len(parts),
        out_specs=[VMEM] * regions,
        out_shape=[jax.ShapeDtypeStruct((used, 2 * rows), jnp.bfloat16)] * regions,
        scratch_shapes=[
            pltpu.VMEM((window, 2 * rows), jnp.float32),
            pltpu.VMEM((used, 2 * rows), jnp.float32),
        ],
        compiler_params=params(),
        cost_estimate=cost(0, 16 * rows * (window + regions * used)),
        name="gather",
    )(picks, *parts)


def stats_kernel(pick_ref, taper_ref, before_ref, value_ref, prec_ref, after_ref, out_ref, table_ref):
    width = before_ref.shape[1]
    cuts = [slice(k, k + LANES) for k in range(0, width, LANES)]
    blocks = [before_ref[-8:, cut] for cut in cuts]
    blank = jnp.zeros((6, LANES), jnp.float32)
    for k in range(0, value_ref.shape[1], LANES):
        cut = slice(k, k + LANES)
        blocks.append(jnp.concatenate([value_ref[:, cut], prec_ref[:, cut], blank], axis=0))
    blocks += [after_ref[-8:, cut] for cut in cuts]
    for k, block in enumerate(blocks):
        table_ref[k * LANES : (k + 1) * LANES, :] = block.T
    step = 16
    used = out_ref.shape[0]
    pos = lax.axis_index("narrow")

    def move(g, carry):
        for u in range(step):
            j = g * step + u
            out_ref[pl.ds(j, 1), :] = table_ref[pl.ds(pick_ref[pos, j], 1), :]
        return carry

    lax.fori_loop(0, used // step, move, 0)
    for k in range(used // LANES):
        cut = slice(k * LANES, (k + 1) * LANES)
        column = jnp.broadcast_to(taper_ref[:, cut], (8, LANES)).T
        lane = lax.broadcasted_iota(jnp.int32, (LANES, 8), 1)
        out_ref[cut, :] = out_ref[cut, :] * jnp.where(lane == 1, column, 1.0)


def stats(picks, taper, parts):
    before, value, _, after = parts
    window = before.shape[1] + value.shape[1] + after.shape[1]
    used = picks.shape[1]
    return pl.pallas_call(
        stats_kernel,
        in_specs=[SMEM] + [VMEM] * (1 + len(parts)),
        out_specs=VMEM,
        out_shape=jax.ShapeDtypeStruct((used, 8), jnp.float32),
        scratch_shapes=[pltpu.VMEM((window, 8), jnp.float32)],
        compiler_params=params(),
        cost_estimate=cost(0, 512 * (window + used)),
        name="stats",
    )(picks, taper, *parts)


def dot(a, b):
    return jnp.dot(a, b, precision=lax.Precision.HIGHEST, preferred_element_type=jnp.float32)


def transform_kernel(own_ref, stats_ref, *refs):
    others, out_ref = refs[:-1], refs[-1]
    ensemble = jnp.concatenate([own_ref[...]] + [r[...] for r in others], axis=1).astype(jnp.float32)
    members = ensemble.shape[1]
    value, weight = stats_ref[:, 0:1], stats_ref[:, 1:2]
    mean = jnp.sum(ensemble, axis=1, keepdims=True) * (1.0 / members)
    pert = ensemble - mean
    scaled = (pert * jnp.sqrt(weight)).astype(jnp.bfloat16)
    forcing = jnp.sum(pert * (weight * (value - mean)), axis=0, keepdims=True)
    row = lax.broadcasted_iota(jnp.int32, (members, members), 0)
    column = lax.broadcasted_iota(jnp.int32, (members, members), 1)
    identity = jnp.where(row == column, 1.0, 0.0)
    matrix = (members - 1.0) * identity + lax.dot_general(
        scaled, scaled, (((0,), (0,)), ((), ())), preferred_element_type=jnp.float32
    )
    squares = jnp.sum(jnp.sum(matrix * matrix, axis=0, keepdims=True), axis=1, keepdims=True)
    norm_scale = jnp.sqrt(squares)
    current = matrix / norm_scale
    root = 1.5 * identity - 0.5 * current
    current = dot(current, root)
    for iteration in range(1, ITERS):
        middle = 1.5 * identity - 0.5 * dot(root, current)
        if iteration < ITERS - 1:
            current = dot(current, middle)
        root = dot(middle, root)
    inv_root = root / jnp.sqrt(norm_scale)
    forcing = jnp.broadcast_to(forcing, (8, members))
    mean_weights = dot(dot(forcing, inv_root), inv_root)[0:1]
    out_ref[...] = (jnp.sqrt(jnp.float32(members - 1)) * inv_root + mean_weights).astype(jnp.bfloat16)


def transform(picked, stat, others):
    used, pair = picked.shape
    members = pair * (1 + len(others))
    return pl.pallas_call(
        transform_kernel,
        grid=(1,),
        in_specs=[
            pl.BlockSpec((used, pair), lambda i: (0, 0)),
            pl.BlockSpec((used, 8), lambda i: (0, 0)),
        ]
        + [pl.BlockSpec((used, pair), lambda i: (0, 0))] * len(others),
        out_specs=pl.BlockSpec((members, members), lambda i: (0, 0)),
        out_shape=jax.ShapeDtypeStruct((members, members), jnp.bfloat16),
        compiler_params=params(),
        cost_estimate=cost(16 * 6 * 2 * members**3, 4 * used * members),
        name="transform",
    )(picked, stat, *others)


def apply_kernel(parts, weights_ref, *refs):
    sources, outs = refs[:parts], refs[-parts:]
    pieces = [r[...].astype(jnp.float32) for r in sources]
    rows = pieces[0].shape[0]
    total = sum(jnp.sum(p, axis=0, keepdims=True) for p in pieces)
    mean = total * (1.0 / (rows * parts))
    pert = jnp.concatenate([(p - mean).astype(jnp.bfloat16) for p in pieces], axis=0)
    mixed = jnp.dot(weights_ref[...], pert, preferred_element_type=jnp.float32)
    result = (mixed + mean).astype(jnp.bfloat16)
    for d in range(parts):
        outs[d][...] = result[d * rows : (d + 1) * rows]


def apply(weights, states, arrived, offsets, result, first, blocks, block, stride):
    rows = states.shape[0]
    width = blocks * block
    parts = len(arrived) + 1
    members = rows * parts

    def far(offset):
        return pl.BlockSpec((rows, block), lambda i: (0, offset + i))

    near = pl.BlockSpec(
        (rows, block), lambda i: (0, lax.axis_index("narrow") * stride + first + i)
    )
    given = [] if result is None else [result]
    return pl.pallas_call(
        functools.partial(apply_kernel, parts),
        grid=(blocks,),
        in_specs=[pl.BlockSpec((members, members), lambda i: (0, 0)), near]
        + [far(offset) for offset in offsets]
        + [HBM] * len(given),
        out_specs=[near] + [far(0)] * (parts - 1),
        out_shape=[jax.ShapeDtypeStruct(states.shape, jnp.bfloat16)]
        + [pltpu.VMEM((rows, width), jnp.bfloat16)] * (parts - 1),
        input_output_aliases={1 + parts: 0} if given else {},
        compiler_params=params(),
        cost_estimate=cost(2 * members * members * width, 4 * members * width),
        name="apply",
    )(weights, states, *arrived, *given)


def place_kernel(cells, start, partners, result_ref, *refs):
    del result_ref
    parts, out_ref, sems = refs[:-2], refs[-2], refs[-1]
    pos = lax.axis_index("narrow")
    copies = []
    for k, part in enumerate(parts):
        column = pl.multiple_of((pos ^ partners[k]) * cells + start, LANES)
        copies.append(
            pltpu.make_async_copy(part, out_ref.at[:, pl.ds(column, part.shape[1])], sems.at[k])
        )
        copies[-1].start()
    for copy in copies:
        copy.wait()


def place(result, parts, cells, start, partners):
    return pl.pallas_call(
        functools.partial(place_kernel, cells, start, partners),
        in_specs=[HBM] + [VMEM] * len(parts),
        out_specs=HBM,
        out_shape=jax.ShapeDtypeStruct(result.shape, result.dtype),
        scratch_shapes=[pltpu.SemaphoreType.DMA((len(parts),))],
        input_output_aliases={0: 0},
        compiler_params=params(),
        cost_estimate=cost(0, sum(4 * p.size for p in parts)),
        name="place",
    )(result, *parts)


def body(states, obs_ens, obs_value, obs_prec, obs_pick, taper):
    n = lax.axis_size("narrow")
    cells = states.shape[1] // n
    unit = cells // 8
    states = pltpu.with_memory_space_constraint(states, pltpu.HBM)

    arrived = {d: [] for d in range(1, n)}

    def send(partners, first, count):
        parts = pack(states, partners, cells, first * unit, count * unit)
        for d, part in zip(partners, parts):
            arrived[d].append((first, count, swap(part, d)))

    far = list(range(2, n))
    send(far[:1], *FIRST[0])
    send(far[1:], *OTHERS[0])
    send(far[:1], *FIRST[1])
    send(far, *OTHERS[1])
    send([1], 0, 8)

    other = swap(obs_ens, 1)
    value, prec = obs_value.reshape(1, -1), obs_prec.reshape(1, -1)
    last, first = edges(obs_ens, value, prec, HALO)
    before, after = halo(last, first, 0)
    other_before, other_after = halo(last, first, 1)
    rows = states.shape[0]
    picked = gather(obs_pick, [before, other_before, obs_ens, other, after, other_after], rows)
    others = []
    for d in far[::2]:
        others.append(swap(picked[d // 2], d))
    stat = stats(obs_pick, taper, [before, value, prec, after])
    weights = transform(picked[0], stat, others)

    result, outgoing = None, []
    for first, count in STEPS:
        parts, offsets = [], []
        for d in range(1, n):
            for base, units, part in arrived[d]:
                if base <= first < base + units:
                    parts.append(part)
                    offsets.append(first - base)
        result, *leaving = apply(
            weights, states, parts, offsets, result, first, count, unit, cells // unit
        )
        moved = []
        for d, part in enumerate(leaving, 1):
            moved.append(swap(part, d))
        outgoing.append((first, moved))
    for first, moved in outgoing:
        cut = n - 1 if first != STEPS[-1][0] else n - 2
        partners = list(range(1, n))
        result = place(result, moved[:cut], cells, first * unit, partners[:cut])
        if cut < n - 1:
            result = place(result, moved[cut:], cells, first * unit, partners[cut:])
    return result


def solution(mesh):
    return jax.shard_map(
        body,
        mesh=mesh,
        in_specs=(
            P("narrow", "wide"),
            P("narrow", "wide"),
            P("wide"),
            P("wide"),
            P("wide", None),
            P(("wide", "narrow"), None),
        ),
        out_specs=P("narrow", "wide"),
        check_vma=False,
    )
```
